32 devices in a mesh: group: 2 (over x), dp: 16 (over z, y, core).
Axes of the slice: x: 2, y: 2, z: 4, core: 2. Of those that a mesh axis runs over, the one named last changes fastest.
Arguments:
- tokens: bfloat16 [512, 4096], P(('group', 'dp')), parts along dimension 0, may hold values from -6 to 6
- cotangent: bfloat16 [512, 8192], P('group', 'dp'), parts along dimension 0, may hold values from -0.75 to 0.75
- token_weight: float32 [512], P('group'), parts along dimension 0, may hold values from 0.5 to 1.5
- weight: bfloat16 [4096, 8192], P(None, 'dp'), may hold values from -0.09375 to 0.09375
- moment_one: bfloat16 [4096, 8192], P(None, 'dp'), may hold values from -6 to 6
- moment_two: bfloat16 [4096, 8192], P(None, 'dp'), may hold values from 0.003 to 10
- adjoint: float32 [4096, 8192], P(None, 'dp'), may hold values from -5 to 5
Outputs:
- theta_bar: float32 [8192, 8192], P('group', 'dp'), parts along dimension 0
- token_scores: float32 [512], P(('group', 'dp')), parts along dimension 0
The draws below stay inside these ranges and needn't reach their ends.
There are 2 independent parts, one for each index of `group`. The reference program is written for one: setup_inputs(seed, part) draws one part's arguments, and reference() takes and returns one part's arrays. A program takes and returns all parts, laid end to end along the dimension named above; an argument that names none is the same for every part. Nothing has to cross between parts.
All inputs are finite; a program needn't handle non-finite values.
Results may differ from the reference program's by a relative error of at most 0.0038.
Values may be sent and summed in bfloat16 or wider, within the bound.
A program may use at most 128 MiB of HBM per device.

```python
import math
import jax
import jax.numpy as jnp
from jax import lax

D = 4096
FW = 8192
TOKENS = 256


def moment_fields(key):
    key = jax.random.fold_in(key, 7)
    key_one, key_rows, key_cols, key_base = jax.random.split(key, 4)
    ln_ten = math.log(10.0)
    one = jax.random.truncated_normal(key_one, -6.0, 6.0, (D, FW), jnp.float32)
    rows = jnp.exp(jax.random.uniform(key_rows, (D, 1), jnp.float32) * ln_ten)
    cols = jnp.exp(jax.random.uniform(key_cols, (1, FW), jnp.float32) * ln_ten)
    base = jnp.exp(jax.random.uniform(key_base, (D, FW), jnp.float32, -1.2, 1.2))
    place = jnp.arange(FW, dtype=jnp.float32)[None, :] / (FW - 1)
    trend = jnp.exp(-math.log(3.0) * place)
    two = 0.03 * base * rows * cols * trend
    return (one, two)


def draw_moment_one(key, part):
    one, two = moment_fields(key)
    return one.astype(jnp.bfloat16)


def draw_moment_two(key, part):
    one, two = moment_fields(key)
    return two.astype(jnp.bfloat16)


def draw_adjoint(key, part):
    one, two = moment_fields(key)
    ratio = one / jnp.sqrt(two + 0.05)
    noise_key = jax.random.fold_in(key, 11)
    along = 1.5 * jnp.tanh(ratio / 3.0)
    noise = 0.8 * jax.random.truncated_normal(noise_key, -4.0, 4.0, (D, FW), jnp.float32)
    return along + noise


def levels(rng, dims, cuts, least, high):
    def one(position, blocks):
        steps = jax.random.uniform(jax.random.fold_in(jax.random.fold_in(rng, 6), position), (blocks,), jnp.float32, least / len(cuts), high / len(cuts))
        return jnp.repeat(jnp.exp(steps), dims[position] // blocks).reshape((-1,) + (1,) * (len(dims) - position - 1))

    factor_of = one(*cuts[0])
    for cut in cuts[1:]:
        factor_of = factor_of * one(*cut)
    return factor_of


def normal_values(key, dims, scale, reach, shards=(), held_as=jnp.bfloat16):
    loudness = levels(key, dims, shards, -0.22, 0.18) if shards else 1.0
    result = jax.random.normal(key, dims, jnp.float32) * scale * loudness
    return jnp.minimum(jnp.maximum(result, -reach), reach).astype(held_as)


def setup_inputs(seed: int = 0, part: int = 0) -> dict:
    seeds = jax.random.split(jax.random.key(seed), 8)
    own_keys = jax.random.split(jax.random.fold_in(seeds[7], part), 8)
    return {
        "tokens": normal_values(own_keys[0], (TOKENS, D), 1.0, 6.0, ((0, 16),)),
        "cotangent": normal_values(own_keys[1], (TOKENS, FW), 0.05, 0.75, ((1, 16),)),
        "token_weight": jnp.clip(jax.random.uniform(own_keys[2], (TOKENS,), jnp.float32, 0.5, 1.5), 0.5, 1.5),
        "weight": normal_values(seeds[3], (D, FW), D ** -0.5, 0.09375, ((1, 16),)),
        "moment_one": draw_moment_one(jax.random.fold_in(seeds[7], 71), part),
        "moment_two": draw_moment_two(jax.random.fold_in(seeds[7], 71), part),
        "adjoint": draw_adjoint(jax.random.fold_in(seeds[7], 71), part),
    }


def slopes(gate):
    sig = jax.nn.sigmoid(gate)
    slope = sig * (1.0 + gate * (1.0 - sig))
    curve = sig * (1.0 - sig) * (2.0 + gate * (1.0 - 2.0 * sig))
    return (slope, curve)

def reference(tokens, cotangent, token_weight, weight, moment_one, moment_two, adjoint):
    gate = jnp.dot(tokens, weight, preferred_element_type=jnp.float32)
    slope, curve = slopes(gate)
    cot_f = cotangent.astype(jnp.float32)
    scaled = (token_weight[:, None] * cot_f * slope).astype(jnp.bfloat16)
    grad = lax.dot_general(tokens, scaled, (((0,), (0,)), ((), ())), preferred_element_type=jnp.float32)
    first = 0.9 * moment_one.astype(jnp.float32) + 0.1 * grad
    second = 0.95 * moment_two.astype(jnp.float32) + 0.05 * grad * grad
    root = jnp.sqrt(second)
    den = root + 1e-08
    upd = first / den
    count = D * FW
    sq = jnp.sum(upd * upd)
    cross = jnp.sum(adjoint * upd)
    rms = jnp.sqrt(sq / count)
    scale = 1.0 / jnp.maximum(1.0, rms)
    bind = jnp.where(rms > 1.0, 1.0 / (rms * rms * rms), 0.0)
    ubar = -0.01 * scale * adjoint + 0.01 * cross * bind / count * upd
    mbar = ubar / den
    vbar = -ubar * first / (den * den) / (2.0 * root)
    gbar = (0.1 * mbar + 0.1 * grad * vbar).astype(jnp.bfloat16)
    probe = jnp.dot(tokens, gbar, preferred_element_type=jnp.float32)
    bent = (token_weight[:, None] * cot_f * curve * probe).astype(jnp.bfloat16)
    theta_bar = 0.999 * adjoint + lax.dot_general(tokens, bent, (((0,), (0,)), ((), ())), preferred_element_type=jnp.float32)
    token_scores = lax.optimization_barrier(jnp.sum(cot_f * slope * probe, axis=1))
    return (theta_bar, token_scores)
```

```python
import functools

import jax
import jax.numpy as jnp
from jax import lax
from jax.experimental import pallas as pl
from jax.experimental.pallas import tpu as pltpu
from jax.sharding import PartitionSpec as P

D = 4096
FW = 8192
COUNT = D * FW
MESH = pl.DeviceIdType.MESH
KB = 256
STRIP = 16


def dot(a, b):
    return jnp.dot(a, b, preferred_element_type=jnp.float32)


def dot_rows(a, b):
    return lax.dot_general(a, b, (((0,), (0,)), ((), ())), preferred_element_type=jnp.float32)


def main_kernel(
    n, wide,
    x_ref, cot_ref, tw_ref, w_hbm, one_hbm, two_hbm, adj_hbm,
    tok_out, bent_out, score_out,
    tok, w, one, two, adj, upd_s, k_s, gate_s, p_s, q_s, scaled_s, probe_s,
    mine, sums, sc, scs,
    load_sem, own_sem, out_sem, gs, gr, ss, sr, cs, cr,
):
    me = lax.axis_index("dp")
    line = n // (2 * wide)
    core = lax.rem(me, 2)
    y = lax.rem(me // 2, wide)
    z = me // (2 * wide)
    stride = 2 * wide
    sibling = me + 1 - 2 * core
    across = me + (1 - 2 * y) * 2
    rows = x_ref.shape[0]
    tokens, width = scaled_s.shape

    loads = [
        pltpu.make_async_copy(src, dst, load_sem.at[i])
        for i, (src, dst) in enumerate(
            ((w_hbm, w), (two_hbm, two), (one_hbm, one), (adj_hbm, adj)))
    ]

    def slab(o):
        return tok.at[pl.ds(pl.multiple_of(o * rows, rows), rows), :]

    own = pltpu.make_async_copy(x_ref, slab(me), own_sem)

    barrier = pltpu.get_barrier_semaphore()

    def greet(k, _):
        pl.semaphore_signal(barrier, inc=1, device_id={"dp": lax.rem(me + k, n)}, device_id_type=MESH)
        return 0

    lax.fori_loop(1, n, greet, 0)
    for copy in loads:
        copy.start()
    own.start()
    pl.semaphore_wait(barrier, n - 1)

    def push(kind, o, dev, src=None):
        return pltpu.make_async_remote_copy(
            src_ref=slab(o) if src is None else src,
            dst_ref=slab(o),
            send_sem=gs.at[kind, o],
            recv_sem=gr.at[o],
            device_id={"dp": dev},
            device_id_type=MESH,
        )

    def arrive(o):
        push(3, o, sibling).wait_recv()

    more, less = z + 1 < line, z > 0

    @pl.when(more)
    def _():
        push(0, me, me + stride, x_ref).start()

    @pl.when(less)
    def _():
        push(1, me, me - stride, x_ref).start()

    if wide == 2:
        push(2, me, across, x_ref).start()
    push(3, me, sibling, x_ref).start()

    def from_across(k):
        if wide != 2:
            return
        for way in (-1, 1) if k else (1,):
            o = across + way * k * stride

            @pl.when((z + way * k >= 0) & (z + way * k < line))
            def _():
                arrive(o)
                push(3, o, sibling).start()

    for k in range(1, line):
        for way, kind, onward in ((-1, 0, more), (1, 1, less)):
            o = me + way * k * stride

            @pl.when((z + way * k >= 0) & (z + way * k < line))
            def _():
                arrive(o)

                @pl.when(onward)
                def _():
                    push(kind, o, me - way * stride).start()

                if wide == 2:
                    push(2, o, across).start()
                push(3, o, sibling).start()

        from_across(k - 1)
    from_across(line - 1)

    def from_sibling(i, _):
        arrive(2 * i + 1 - core)
        return 0

    lax.fori_loop(0, n // 2, from_sibling, 0)
    own.wait()
    keep = pltpu.make_async_copy(tok, tok_out, out_sem)
    keep.start()

    loads[0].wait()
    gate_s[...] = jnp.zeros_like(gate_s)

    def gate_step(i, _):
        ks = pl.ds(pl.multiple_of(i * 512, 512), 512)
        gate_s[...] += dot(tok[:, ks], w[ks, :])
        return 0

    lax.fori_loop(0, D // 512, gate_step, 0)

    tw = jnp.transpose(jnp.broadcast_to(tw_ref[...], (128, tokens)))
    q_s[:, 0:128] = tw

    def slope_step(i, _):
        rs = pl.ds(pl.multiple_of(i * STRIP, STRIP), STRIP)
        tw = q_s[rs, 0:128]
        for j in range(width // 128):
            js = slice(j * 128, (j + 1) * 128)
            gate = gate_s[rs, js]
            cot = cot_ref[rs, js].astype(jnp.float32)
            sig = jax.nn.sigmoid(gate)
            slope = sig * (1.0 + gate * (1.0 - sig))
            curve = sig * (1.0 - sig) * (2.0 + gate * (1.0 - 2.0 * sig))
            scaled_s[rs, js] = (tw * cot * slope).astype(jnp.bfloat16)
            p_s[rs, js] = cot * slope
            q_s[rs, js] = tw * cot * curve
        return 0

    lax.fori_loop(0, tokens // STRIP, slope_step, 0, unroll=4)

    for copy in loads[1:]:
        copy.wait()

    def fold(v):
        out = None
        for i in range(v.shape[0] // 8):
            for j in range(width // 128):
                part = v[i * 8:(i + 1) * 8, j * 128:(j + 1) * 128]
                out = part if out is None else out + part
        return out

    def grad_step(i, carry):
        sq, cross = carry
        base = pl.multiple_of(i * KB, KB)
        g_all = dot_rows(tok[:, pl.ds(base, KB)], scaled_s[...])
        for r in range(0, KB, STRIP):
            rs = pl.ds(pl.multiple_of(base + r, STRIP), STRIP)
            g = g_all[r:r + STRIP]
            first = 0.9 * one[rs, :].astype(jnp.float32) + 0.1 * g
            second = 0.95 * two[rs, :].astype(jnp.float32) + 0.05 * g * g
            inv_root = lax.rsqrt(second)
            den = second * inv_root + 1e-08
            inv = lax.rsqrt(den * den)
            upd = first * inv
            upd_s[rs, :] = upd
            k_s[rs, :] = (0.1 * inv) * (1.0 - 0.5 * (g * upd) * inv_root)
            sq = sq + fold(upd * upd)
            cross = cross + fold(adj[rs, :] * upd)
        return sq, cross

    zero = jnp.zeros((8, 128), jnp.float32)
    sq, cross = lax.fori_loop(0, D // KB, grad_step, (zero, zero))
    mine[0] = sq
    mine[1] = cross
    sums[me, 0] = sq
    sums[me, 1] = cross

    def sum_copy(k):
        return pltpu.make_async_remote_copy(
            src_ref=mine, dst_ref=sums.at[me],
            send_sem=ss.at[k], recv_sem=sr.at[me],
            device_id={"dp": lax.rem(me + k, n)}, device_id_type=MESH)

    def sum_arrive(k):
        o = lax.rem(me + k, n)
        pltpu.make_async_remote_copy(
            src_ref=mine, dst_ref=sums.at[o],
            send_sem=ss.at[k], recv_sem=sr.at[o],
            device_id={"dp": o}, device_id_type=MESH).wait_recv()

    def each(body):
        def step(k, _):
            body(k)
            return 0

        lax.fori_loop(1, n, step, 0)

    each(lambda k: sum_copy(k).start())
    probe_s[...] = jnp.zeros_like(probe_s)
    each(sum_arrive)

    tot = sums[0]
    for o in range(1, n):
        tot = tot + sums[o]
    sq = jnp.sum(tot[0], keepdims=True)
    cross = jnp.sum(tot[1], keepdims=True)
    rms = jnp.sqrt(sq / COUNT)
    scale = 1.0 / jnp.maximum(1.0, rms)
    bind = jnp.where(rms > 1.0, 1.0 / (rms * rms * rms), 0.0)
    alpha = jnp.broadcast_to(-0.01 * scale, (STRIP, width))
    beta = jnp.broadcast_to(0.01 * cross * bind / COUNT, (STRIP, width))

    def probe_step(i, _):
        base = pl.multiple_of(i * 512, 512)
        parts = []
        for r in range(0, 512, STRIP):
            rs = pl.ds(pl.multiple_of(base + r, STRIP), STRIP)
            ubar = alpha * adj[rs, :] + beta * upd_s[rs, :]
            parts.append((ubar * k_s[rs, :]).astype(jnp.bfloat16))
        probe_s[...] += dot(tok[:, pl.ds(base, 512)], jnp.concatenate(parts, axis=0))
        return 0

    lax.fori_loop(0, D // 512, probe_step, 0)

    def score_step(i, _):
        rs = pl.ds(pl.multiple_of(i * STRIP, STRIP), STRIP)
        out = None
        for j in range(width // 128):
            js = slice(j * 128, (j + 1) * 128)
            part = p_s[rs, js] * probe_s[rs, js]
            out = part if out is None else out + part
        sc[rs, :] = out
        return 0

    lax.fori_loop(0, tokens // STRIP, score_step, 0, unroll=4)

    def sc_rows(o):
        return sc.at[pl.ds(pl.multiple_of(o * rows, rows), rows), :]

    scs[me] = sc[pl.ds(pl.multiple_of(me * rows, rows), rows), :]

    def score_copy(k):
        o = lax.rem(me + k, n)
        return pltpu.make_async_remote_copy(
            src_ref=sc_rows(o), dst_ref=scs.at[me],
            send_sem=cs.at[k], recv_sem=cr.at[me],
            device_id={"dp": o}, device_id_type=MESH)

    def score_arrive(k):
        o = lax.rem(me + k, n)
        pltpu.make_async_remote_copy(
            src_ref=sc_rows(o), dst_ref=scs.at[o],
            send_sem=cs.at[k], recv_sem=cr.at[o],
            device_id={"dp": o}, device_id_type=MESH).wait_recv()

    each(lambda k: score_copy(k).start())

    def bent_step(i, _):
        rs = pl.ds(pl.multiple_of(i * STRIP, STRIP), STRIP)
        bent_out[rs, :] = (q_s[rs, :] * probe_s[rs, :]).astype(jnp.bfloat16)
        return 0

    lax.fori_loop(0, tokens // STRIP, bent_step, 0, unroll=4)

    def sent_line(i, _):
        o = (i * wide + y) * 2 + core

        @pl.when((i <= z) & more)
        def _():
            push(0, o, me + stride).wait_send()

        @pl.when((i >= z) & less)
        def _():
            push(1, o, me - stride).wait_send()

        if wide == 2:
            push(2, o, across).wait_send()
        return 0

    lax.fori_loop(0, line, sent_line, 0)

    def sent_core(i, _):
        push(3, 2 * i + core, sibling).wait_send()
        return 0

    lax.fori_loop(0, n // 2, sent_core, 0)
    each(lambda k: sum_copy(k).wait_send())
    each(score_arrive)
    tot = scs[0]
    for o in range(1, n):
        tot = tot + scs[o]
    score_out[...] = tot
    each(lambda k: score_copy(k).wait_send())
    keep.wait()


def last_kernel(tok_ref, bent_ref, adj_ref, sc_ref, theta_ref, score_ref):
    theta_ref[...] = 0.999 * adj_ref[...] + dot_rows(tok_ref[...], bent_ref[...])

    @pl.when(pl.program_id(0) == 0)
    def _():
        rows = sc_ref.shape[0]
        total = jnp.sum(sc_ref[...], axis=1, keepdims=True)
        at = lax.broadcasted_iota(jnp.int32, (rows, 128), 0)
        lane = lax.broadcasted_iota(jnp.int32, (rows, 128), 1)
        row = jnp.sum(jnp.where(at == lane, total, 0.0), axis=0, keepdims=True)
        score_ref[...] = row[:, :rows]


def shards(n, wide, x, cotangent, token_weight, weight, moment_one, moment_two, adjoint):
    rows = x.shape[0]
    tokens = n * rows
    width = weight.shape[1]
    f32, bf16 = jnp.float32, jnp.bfloat16
    vm = pl.BlockSpec(memory_space=pltpu.VMEM)
    hbm = pl.BlockSpec(memory_space=pl.ANY)
    dma = pltpu.SemaphoreType.DMA
    tok, bent, sc = pl.pallas_call(
        functools.partial(main_kernel, n, wide),
        out_shape=(
            jax.ShapeDtypeStruct((tokens, D), bf16),
            jax.ShapeDtypeStruct((tokens, width), bf16),
            jax.ShapeDtypeStruct((rows, 128), f32),
        ),
        in_specs=[hbm, vm, vm, hbm, hbm, hbm, hbm],
        out_specs=(hbm, vm, vm),
        scratch_shapes=[
            pltpu.VMEM((tokens, D), bf16),
            pltpu.VMEM((D, width), bf16),
            pltpu.VMEM((D, width), bf16),
            pltpu.VMEM((D, width), bf16),
            pltpu.VMEM((D, width), f32),
            pltpu.VMEM((D, width), f32),
            pltpu.VMEM((D, width), f32),
            pltpu.VMEM((tokens, width), f32),
            pltpu.VMEM((tokens, width), f32),
            pltpu.VMEM((tokens, width), f32),
            pltpu.VMEM((tokens, width), bf16),
            pltpu.VMEM((tokens, width), f32),
            pltpu.VMEM((2, 8, 128), f32),
            pltpu.VMEM((n, 2, 8, 128), f32),
            pltpu.VMEM((tokens, 128), f32),
            pltpu.VMEM((n, rows, 128), f32),
            dma((4,)),
            dma,
            dma,
            dma((4, n)),
            dma((n,)),
            dma((n,)),
            dma((n,)),
            dma((n,)),
            dma((n,)),
        ],
        compiler_params=pltpu.CompilerParams(
            collective_id=0, has_side_effects=True, vmem_limit_bytes=60 * 2**20
        ),
    )(x, cotangent, token_weight.reshape(1, tokens), weight, moment_one, moment_two, adjoint)
    step = 512
    theta, score = pl.pallas_call(
        last_kernel,
        grid=(D // step,),
        out_shape=(
            jax.ShapeDtypeStruct((D, width), f32),
            jax.ShapeDtypeStruct((1, rows), f32),
        ),
        in_specs=[
            pl.BlockSpec((tokens, step), lambda i: (0, i)),
            pl.BlockSpec((tokens, width), lambda i: (0, 0)),
            pl.BlockSpec((step, width), lambda i: (i, 0)),
            pl.BlockSpec((rows, 128), lambda i: (0, 0)),
        ],
        out_specs=(
            pl.BlockSpec((step, width), lambda i: (i, 0)),
            pl.BlockSpec((1, rows), lambda i: (0, 0)),
        ),
    )(tok, bent, adjoint, sc)
    return theta, score.reshape(rows)


def solution(mesh):
    n = mesh.shape["dp"]
    wide = 2 if mesh.shape["group"] == 2 else 1
    in_specs = (
        P(("group", "dp"), None),
        P("group", "dp"),
        P("group"),
        P(None, "dp"),
        P(None, "dp"),
        P(None, "dp"),
        P(None, "dp"),
    )
    out_specs = (P("group", "dp"), P(("group", "dp")))
    return jax.shard_map(
        functools.partial(shards, n, wide), mesh=mesh,
        in_specs=in_specs, out_specs=out_specs, check_vma=False)
```

```python
import functools

import jax
import jax.numpy as jnp
from jax import lax
from jax.experimental import pallas as pl
from jax.experimental.pallas import tpu as pltpu
from jax.sharding import PartitionSpec as P

D = 4096
FW = 8192
COUNT = D * FW
MESH = pl.DeviceIdType.MESH
KB = 256
STRIP = 16
PIECES = 1
LAST = 8


def dot(a, b):
    return jnp.dot(a, b, preferred_element_type=jnp.float32)


def dot_rows(a, b):
    return lax.dot_general(a, b, (((0,), (0,)), ((), ())), preferred_element_type=jnp.float32)


def main_kernel(
    n, wide,
    x_ref, cot_ref, tw_ref, w_hbm, one_hbm, two_hbm, adj_hbm,
    tok_out, bent_out, score_out,
    tok, w, one, two, adj, upd_s, k_s, gate_s, p_s, q_s, scaled_s, probe_s,
    mine, sums, sc, scs,
    load_sem, own_sem, out_sem, gs, gr, ss, sr, cs, cr,
):
    me = lax.axis_index("dp")
    line = n // (2 * wide)
    core = lax.rem(me, 2)
    y = lax.rem(me // 2, wide)
    z = me // (2 * wide)
    stride = 2 * wide
    sibling = me + 1 - 2 * core
    across = me + (1 - 2 * y) * 2
    rows = x_ref.shape[0]
    tokens, width = scaled_s.shape

    loads = [
        pltpu.make_async_copy(src, dst, load_sem.at[i])
        for i, (src, dst) in enumerate(
            ((w_hbm, w), (two_hbm, two), (one_hbm, one), (adj_hbm, adj)))
    ]

    cols = D // PIECES

    def slab(o, h):
        return tok.at[pl.ds(pl.multiple_of(o * rows, rows), rows), pl.ds(h * cols, cols)]

    own = pltpu.make_async_copy(x_ref, tok.at[pl.ds(pl.multiple_of(me * rows, rows), rows), :], own_sem)

    barrier = pltpu.get_barrier_semaphore()

    def greet(k, _):
        pl.semaphore_signal(barrier, inc=1, device_id={"dp": lax.rem(me + k, n)}, device_id_type=MESH)
        return 0

    lax.fori_loop(1, n, greet, 0)
    for copy in loads:
        copy.start()
    own.start()
    pl.semaphore_wait(barrier, n - 1)

    def push(kind, o, dev, h, src=None):
        return pltpu.make_async_remote_copy(
            src_ref=slab(o, h) if src is None else src.at[:, pl.ds(h * cols, cols)],
            dst_ref=slab(o, h),
            send_sem=gs.at[kind, h, o],
            recv_sem=gr.at[h, o],
            device_id={"dp": dev},
            device_id_type=MESH,
        )

    def arrive(o, h):
        push(3, o, sibling, h).wait_recv()

    more, less = z + 1 < line, z > 0

    for h in range(PIECES):
        @pl.when(more)
        def _():
            push(0, me, me + stride, h, x_ref).start()

        @pl.when(less)
        def _():
            push(1, me, me - stride, h, x_ref).start()

        if wide == 2:
            push(2, me, across, h, x_ref).start()
        push(3, me, sibling, h, x_ref).start()

    def from_across(k, h):
        if wide != 2:
            return
        for way in (-1, 1) if k else (1,):
            o = across + way * k * stride

            @pl.when((z + way * k >= 0) & (z + way * k < line))
            def _():
                arrive(o, h)
                push(3, o, sibling, h).start()

    for k in range(1, line):
        for h in range(PIECES):
            for way, kind, onward in ((-1, 0, more), (1, 1, less)):
                o = me + way * k * stride

                @pl.when((z + way * k >= 0) & (z + way * k < line))
                def _():
                    arrive(o, h)

                    @pl.when(onward)
                    def _():
                        push(kind, o, me - way * stride, h).start()

                    if wide == 2:
                        push(2, o, across, h).start()
                    push(3, o, sibling, h).start()

            from_across(k - 1, h)
    for h in range(PIECES):
        from_across(line - 1, h)

    def from_sibling(i, _):
        for h in range(PIECES):
            arrive(2 * i + 1 - core, h)
        return 0

    lax.fori_loop(0, n // 2, from_sibling, 0)
    own.wait()
    keep = pltpu.make_async_copy(tok, tok_out, out_sem)
    keep.start()

    loads[0].wait()
    gate_s[...] = jnp.zeros_like(gate_s)

    def gate_step(i, _):
        ks = pl.ds(pl.multiple_of(i * 512, 512), 512)
        gate_s[...] += dot(tok[:, ks], w[ks, :])
        return 0

    lax.fori_loop(0, D // 512, gate_step, 0)

    tw = jnp.transpose(jnp.broadcast_to(tw_ref[...], (128, tokens)))
    q_s[:, 0:128] = tw

    def slope_step(i, _):
        rs = pl.ds(pl.multiple_of(i * STRIP, STRIP), STRIP)
        tw = q_s[rs, 0:128]
        for j in range(width // 128):
            js = slice(j * 128, (j + 1) * 128)
            gate = gate_s[rs, js]
            cot = cot_ref[rs, js].astype(jnp.float32)
            sig = jax.nn.sigmoid(gate)
            slope = sig * (1.0 + gate * (1.0 - sig))
            curve = sig * (1.0 - sig) * (2.0 + gate * (1.0 - 2.0 * sig))
            scaled_s[rs, js] = (tw * cot * slope).astype(jnp.bfloat16)
            p_s[rs, js] = cot * slope
            q_s[rs, js] = tw * cot * curve
        return 0

    lax.fori_loop(0, tokens // STRIP, slope_step, 0, unroll=4)

    for copy in loads[1:]:
        copy.wait()

    def fold(v):
        out = None
        for i in range(v.shape[0] // 8):
            for j in range(width // 128):
                part = v[i * 8:(i + 1) * 8, j * 128:(j + 1) * 128]
                out = part if out is None else out + part
        return out

    def grad_step(i, carry):
        sq, cross = carry
        base = pl.multiple_of(i * KB, KB)
        g_all = dot_rows(tok[:, pl.ds(base, KB)], scaled_s[...])
        for r in range(0, KB, STRIP):
            rs = pl.ds(pl.multiple_of(base + r, STRIP), STRIP)
            g = g_all[r:r + STRIP]
            first = 0.9 * one[rs, :].astype(jnp.float32) + 0.1 * g
            second = 0.95 * two[rs, :].astype(jnp.float32) + 0.05 * g * g
            inv_root = lax.rsqrt(second)
            den = second * inv_root + 1e-08
            inv = lax.rsqrt(den * den)
            upd = first * inv
            upd_s[rs, :] = upd
            k_s[rs, :] = (0.1 * inv) * (1.0 - 0.5 * (g * upd) * inv_root)
            sq = sq + fold(upd * upd)
            cross = cross + fold(adj[rs, :] * upd)
        return sq, cross

    zero = jnp.zeros((8, 128), jnp.float32)
    sq, cross = lax.fori_loop(0, D // KB, grad_step, (zero, zero))
    pair = jnp.concatenate(
        [jnp.sum(sq, axis=0, keepdims=True), jnp.sum(cross, axis=0, keepdims=True)], axis=0)
    mine[...] = pair
    sums[me] = pair

    def sum_copy(k):
        return pltpu.make_async_remote_copy(
            src_ref=mine, dst_ref=sums.at[me],
            send_sem=ss.at[k], recv_sem=sr.at[me],
            device_id={"dp": lax.rem(me + k, n)}, device_id_type=MESH)

    def sum_arrive(k):
        o = lax.rem(me + k, n)
        pltpu.make_async_remote_copy(
            src_ref=mine, dst_ref=sums.at[o],
            send_sem=ss.at[k], recv_sem=sr.at[o],
            device_id={"dp": o}, device_id_type=MESH).wait_recv()

    def each(body):
        def step(k, _):
            body(k)
            return 0

        lax.fori_loop(1, n, step, 0)

    each(lambda k: sum_copy(k).start())
    probe_s[...] = jnp.zeros_like(probe_s)
    each(sum_arrive)

    tot = sums[0]
    for o in range(1, n):
        tot = tot + sums[o]
    sq = jnp.sum(tot[0:1], keepdims=True)
    cross = jnp.sum(tot[1:2], keepdims=True)
    rms = jnp.sqrt(sq / COUNT)
    scale = 1.0 / jnp.maximum(1.0, rms)
    bind = jnp.where(rms > 1.0, 1.0 / (rms * rms * rms), 0.0)
    alpha = jnp.broadcast_to(-0.01 * scale, (STRIP, width))
    beta = jnp.broadcast_to(0.01 * cross * bind / COUNT, (STRIP, width))

    def probe_step(i, _):
        base = pl.multiple_of(i * 512, 512)
        parts = []
        for r in range(0, 512, STRIP):
            rs = pl.ds(pl.multiple_of(base + r, STRIP), STRIP)
            ubar = alpha * adj[rs, :] + beta * upd_s[rs, :]
            parts.append((ubar * k_s[rs, :]).astype(jnp.bfloat16))
        probe_s[...] += dot(tok[:, pl.ds(base, 512)], jnp.concatenate(parts, axis=0))
        return 0

    lax.fori_loop(0, D // 512, probe_step, 0)

    at = lax.broadcasted_iota(jnp.int32, (rows, 128), 0)
    lane = lax.broadcasted_iota(jnp.int32, (rows, 128), 1)

    def score_step(i, _):
        rs = pl.ds(pl.multiple_of(i * rows, rows), rows)
        out = None
        for j in range(width // 128):
            js = slice(j * 128, (j + 1) * 128)
            part = p_s[rs, js] * probe_s[rs, js]
            out = part if out is None else out + part
        total = jnp.sum(out, axis=1, keepdims=True)
        sc[i] = jnp.sum(jnp.where(at == lane, total, 0.0), axis=0, keepdims=True)
        return 0

    lax.fori_loop(0, n, score_step, 0, unroll=4)

    def sc_rows(o):
        return sc.at[o]

    scs[me] = sc[me]

    def score_copy(k):
        o = lax.rem(me + k, n)
        return pltpu.make_async_remote_copy(
            src_ref=sc_rows(o), dst_ref=scs.at[me],
            send_sem=cs.at[k], recv_sem=cr.at[me],
            device_id={"dp": o}, device_id_type=MESH)

    def score_arrive(k):
        o = lax.rem(me + k, n)
        pltpu.make_async_remote_copy(
            src_ref=sc_rows(o), dst_ref=scs.at[o],
            send_sem=cs.at[k], recv_sem=cr.at[o],
            device_id={"dp": o}, device_id_type=MESH).wait_recv()

    each(lambda k: score_copy(k).start())

    def bent_step(i, _):
        rs = pl.ds(pl.multiple_of(i * STRIP, STRIP), STRIP)
        bent_out[rs, :] = (q_s[rs, :] * probe_s[rs, :]).astype(jnp.bfloat16)
        return 0

    lax.fori_loop(0, tokens // STRIP, bent_step, 0, unroll=4)

    def sent_line(i, _):
        o = (i * wide + y) * 2 + core
        for h in range(PIECES):
            @pl.when((i <= z) & more)
            def _():
                push(0, o, me + stride, h).wait_send()

            @pl.when((i >= z) & less)
            def _():
                push(1, o, me - stride, h).wait_send()

            if wide == 2:
                push(2, o, across, h).wait_send()
        return 0

    lax.fori_loop(0, line, sent_line, 0)

    def sent_core(i, _):
        for h in range(PIECES):
            push(3, 2 * i + core, sibling, h).wait_send()
        return 0

    lax.fori_loop(0, n // 2, sent_core, 0)
    each(lambda k: sum_copy(k).wait_send())
    each(score_arrive)
    tot = scs[0]
    for o in range(1, n):
        tot = tot + scs[o]
    score_out[...] = tot
    each(lambda k: score_copy(k).wait_send())
    keep.wait()


def last_kernel(tok_hbm, bent_ref, adj_hbm, sc_ref, theta_hbm, score_ref, tok, adj, theta, tok_sem, adj_sem, out_sem):
    step = D // LAST
    parts = [pl.ds(i * step, step) for i in range(LAST)]
    toks = [pltpu.make_async_copy(tok_hbm.at[:, p], tok.at[:, p], tok_sem.at[i]) for i, p in enumerate(parts)]
    adjs = [pltpu.make_async_copy(adj_hbm.at[p, :], adj.at[p, :], adj_sem.at[i]) for i, p in enumerate(parts)]
    outs = [pltpu.make_async_copy(theta.at[p, :], theta_hbm.at[p, :], out_sem.at[i]) for i, p in enumerate(parts)]
    for i in range(LAST):
        toks[i].start()
        adjs[i].start()

    score_ref[...] = sc_ref[:, :score_ref.shape[1]]

    for i, p in enumerate(parts):
        toks[i].wait()
        adjs[i].wait()
        theta[p, :] = 0.999 * adj[p, :] + dot_rows(tok[:, p], bent_ref[...])
        outs[i].start()
    for copy in outs:
        copy.wait()


def shards(n, wide, x, cotangent, token_weight, weight, moment_one, moment_two, adjoint):
    rows = x.shape[0]
    tokens = n * rows
    width = weight.shape[1]
    f32, bf16 = jnp.float32, jnp.bfloat16
    vm = pl.BlockSpec(memory_space=pltpu.VMEM)
    hbm = pl.BlockSpec(memory_space=pl.ANY)
    dma = pltpu.SemaphoreType.DMA
    tok, bent, sc = pl.pallas_call(
        functools.partial(main_kernel, n, wide),
        out_shape=(
            jax.ShapeDtypeStruct((tokens, D), bf16),
            jax.ShapeDtypeStruct((tokens, width), bf16),
            jax.ShapeDtypeStruct((1, 128), f32),
        ),
        in_specs=[hbm, vm, vm, hbm, hbm, hbm, hbm],
        out_specs=(hbm, vm, vm),
        scratch_shapes=[
            pltpu.VMEM((tokens, D), bf16),
            pltpu.VMEM((D, width), bf16),
            pltpu.VMEM((D, width), bf16),
            pltpu.VMEM((D, width), bf16),
            pltpu.VMEM((D, width), f32),
            pltpu.VMEM((D, width), f32),
            pltpu.VMEM((D, width), f32),
            pltpu.VMEM((tokens, width), f32),
            pltpu.VMEM((tokens, width), f32),
            pltpu.VMEM((tokens, width), f32),
            pltpu.VMEM((tokens, width), bf16),
            pltpu.VMEM((tokens, width), f32),
            pltpu.VMEM((2, 128), f32),
            pltpu.VMEM((n, 2, 128), f32),
            pltpu.VMEM((n, 1, 128), f32),
            pltpu.VMEM((n, 1, 128), f32),
            dma((4,)),
            dma,
            dma,
            dma((4, PIECES, n)),
            dma((PIECES, n)),
            dma((n,)),
            dma((n,)),
            dma((n,)),
            dma((n,)),
        ],
        compiler_params=pltpu.CompilerParams(
            collective_id=0, has_side_effects=True, vmem_limit_bytes=60 * 2**20
        ),
    )(x, cotangent, token_weight.reshape(1, tokens), weight, moment_one, moment_two, adjoint)
    theta, score = pl.pallas_call(
        last_kernel,
        out_shape=(
            jax.ShapeDtypeStruct((D, width), f32),
            jax.ShapeDtypeStruct((1, rows), f32),
        ),
        in_specs=[hbm, vm, hbm, vm],
        out_specs=(hbm, vm),
        scratch_shapes=[
            pltpu.VMEM((tokens, D), bf16),
            pltpu.VMEM((D, width), f32),
            pltpu.VMEM((D, width), f32),
            dma((LAST,)),
            dma((LAST,)),
            dma((LAST,)),
        ],
        compiler_params=pltpu.CompilerParams(vmem_limit_bytes=60 * 2**20),
    )(tok, bent, adjoint, sc)
    return theta, score.reshape(rows)


def solution(mesh):
    n = mesh.shape["dp"]
    wide = 2 if mesh.shape["group"] == 2 else 1
    in_specs = (
        P(("group", "dp"), None),
        P("group", "dp"),
        P("group"),
        P(None, "dp"),
        P(None, "dp"),
        P(None, "dp"),
        P(None, "dp"),
    )
    out_specs = (P("group", "dp"), P(("group", "dp")))
    return jax.shard_map(
        functools.partial(shards, n, wide), mesh=mesh,
        in_specs=in_specs, out_specs=out_specs, check_vma=False)
```

```python
import functools

import jax
import jax.numpy as jnp
from jax import lax
from jax.experimental import pallas as pl
from jax.experimental.pallas import tpu as pltpu
from jax.sharding import PartitionSpec as P

D = 4096
FW = 8192
COUNT = D * FW
MESH = pl.DeviceIdType.MESH
KB = 256
STRIP = 16
PIECES = 1
LAST = 8


def dot(a, b):
    return jnp.dot(a, b, preferred_element_type=jnp.float32)


def dot_rows(a, b):
    return lax.dot_general(a, b, (((0,), (0,)), ((), ())), preferred_element_type=jnp.float32)


def main_kernel(
    n, wide,
    x_ref, cot_ref, tw_ref, w_hbm, one_hbm, two_hbm, adj_hbm,
    tok_out, bent_out, score_out,
    tok, w, one, two, adj, upd_s, k_s, gate_s, p_s, q_s, scaled_s, probe_s,
    mine, sums, sc, scs,
    load_sem, own_sem, out_sem, gs, gr, ss, sr, cs, cr,
):
    me = lax.axis_index("dp")
    line = n // (2 * wide)
    core = lax.rem(me, 2)
    y = lax.rem(me // 2, wide)
    z = me // (2 * wide)
    stride = 2 * wide
    sibling = me + 1 - 2 * core
    across = me + (1 - 2 * y) * 2
    rows = x_ref.shape[0]
    tokens, width = scaled_s.shape

    loads = [
        pltpu.make_async_copy(src, dst, load_sem.at[i])
        for i, (src, dst) in enumerate(
            ((w_hbm, w), (two_hbm, two), (one_hbm, one), (adj_hbm, adj)))
    ]

    cols = D // PIECES

    def slab(o, h):
        return tok.at[pl.ds(pl.multiple_of(o * rows, rows), rows), pl.ds(h * cols, cols)]

    own = pltpu.make_async_copy(x_ref, tok.at[pl.ds(pl.multiple_of(me * rows, rows), rows), :], own_sem)

    barrier = pltpu.get_barrier_semaphore()

    def greet(k, _):
        pl.semaphore_signal(barrier, inc=1, device_id={"dp": lax.rem(me + k, n)}, device_id_type=MESH)
        return 0

    lax.fori_loop(1, n, greet, 0)
    for copy in loads:
        copy.start()
    own.start()
    pl.semaphore_wait(barrier, n - 1)

    def push(kind, o, dev, h, src=None):
        return pltpu.make_async_remote_copy(
            src_ref=slab(o, h) if src is None else src.at[:, pl.ds(h * cols, cols)],
            dst_ref=slab(o, h),
            send_sem=gs.at[kind, h, o],
            recv_sem=gr.at[h, o],
            device_id={"dp": dev},
            device_id_type=MESH,
        )

    def direct(dev, h):
        return pltpu.make_async_remote_copy(
            src_ref=x_ref.at[:, pl.ds(h * cols, cols)],
            dst_ref=slab(me, h),
            send_sem=gs.at[0, h, dev],
            recv_sem=gr.at[h, me],
            device_id={"dp": dev},
            device_id_type=MESH,
        )

    def arrive(o, h):
        push(3, o, sibling, h).wait_recv()

    for h in range(PIECES):
        for k in range(1, line):
            for way in (-1, 1):
                @pl.when((z + way * k >= 0) & (z + way * k < line))
                def _():
                    direct(me + way * k * stride, h).start()

        if wide == 2:
            push(2, me, across, h, x_ref).start()
        push(3, me, sibling, h, x_ref).start()

    def from_across(k, h):
        if wide != 2:
            return
        for way in (-1, 1) if k else (1,):
            o = across + way * k * stride

            @pl.when((z + way * k >= 0) & (z + way * k < line))
            def _():
                arrive(o, h)
                push(3, o, sibling, h).start()

    for k in range(1, line):
        for h in range(PIECES):
            for way in (-1, 1):
                o = me + way * k * stride

                @pl.when((z + way * k >= 0) & (z + way * k < line))
                def _():
                    arrive(o, h)

                    if wide == 2:
                        push(2, o, across, h).start()
                    push(3, o, sibling, h).start()

            from_across(k - 1, h)
    for h in range(PIECES):
        from_across(line - 1, h)

    def from_sibling(i, _):
        for h in range(PIECES):
            arrive(2 * i + 1 - core, h)
        return 0

    lax.fori_loop(0, n // 2, from_sibling, 0)
    own.wait()
    keep = pltpu.make_async_copy(tok, tok_out, out_sem)
    keep.start()

    loads[0].wait()
    gate_s[...] = jnp.zeros_like(gate_s)

    def gate_step(i, _):
        ks = pl.ds(pl.multiple_of(i * 512, 512), 512)
        gate_s[...] += dot(tok[:, ks], w[ks, :])
        return 0

    lax.fori_loop(0, D // 512, gate_step, 0)

    tw = jnp.transpose(jnp.broadcast_to(tw_ref[...], (128, tokens)))
    q_s[:, 0:128] = tw

    def slope_step(i, _):
        rs = pl.ds(pl.multiple_of(i * STRIP, STRIP), STRIP)
        tw = q_s[rs, 0:128]
        for j in range(width // 128):
            js = slice(j * 128, (j + 1) * 128)
            gate = gate_s[rs, js]
            cot = cot_ref[rs, js].astype(jnp.float32)
            sig = jax.nn.sigmoid(gate)
            slope = sig * (1.0 + gate * (1.0 - sig))
            curve = sig * (1.0 - sig) * (2.0 + gate * (1.0 - 2.0 * sig))
            scaled_s[rs, js] = (tw * cot * slope).astype(jnp.bfloat16)
            p_s[rs, js] = cot * slope
            q_s[rs, js] = tw * cot * curve
        return 0

    lax.fori_loop(0, tokens // STRIP, slope_step, 0, unroll=4)

    for copy in loads[1:]:
        copy.wait()

    def fold(v):
        out = None
        for i in range(v.shape[0] // 8):
            for j in range(width // 128):
                part = v[i * 8:(i + 1) * 8, j * 128:(j + 1) * 128]
                out = part if out is None else out + part
        return out

    def grad_step(i, carry):
        sq, cross = carry
        base = pl.multiple_of(i * KB, KB)
        g_all = dot_rows(tok[:, pl.ds(base, KB)], scaled_s[...])
        for r in range(0, KB, STRIP):
            rs = pl.ds(pl.multiple_of(base + r, STRIP), STRIP)
            g = g_all[r:r + STRIP]
            first = 0.9 * one[rs, :].astype(jnp.float32) + 0.1 * g
            second = 0.95 * two[rs, :].astype(jnp.float32) + 0.05 * g * g
            inv_root = lax.rsqrt(second)
            den = second * inv_root + 1e-08
            inv = lax.rsqrt(den * den)
            upd = first * inv
            upd_s[rs, :] = upd
            k_s[rs, :] = (0.1 * inv) * (1.0 - 0.5 * (g * upd) * inv_root)
            sq = sq + fold(upd * upd)
            cross = cross + fold(adj[rs, :] * upd)
        return sq, cross

    zero = jnp.zeros((8, 128), jnp.float32)
    sq, cross = lax.fori_loop(0, D // KB, grad_step, (zero, zero))
    pair = jnp.concatenate(
        [jnp.sum(sq, axis=0, keepdims=True), jnp.sum(cross, axis=0, keepdims=True)], axis=0)
    mine[...] = pair
    sums[me] = pair

    def sum_copy(k):
        return pltpu.make_async_remote_copy(
            src_ref=mine, dst_ref=sums.at[me],
            send_sem=ss.at[k], recv_sem=sr.at[me],
            device_id={"dp": lax.rem(me + k, n)}, device_id_type=MESH)

    def sum_arrive(k):
        o = lax.rem(me + k, n)
        pltpu.make_async_remote_copy(
            src_ref=mine, dst_ref=sums.at[o],
            send_sem=ss.at[k], recv_sem=sr.at[o],
            device_id={"dp": o}, device_id_type=MESH).wait_recv()

    def each(body):
        def step(k, _):
            body(k)
            return 0

        lax.fori_loop(1, n, step, 0)

    each(lambda k: sum_copy(k).start())
    probe_s[...] = jnp.zeros_like(probe_s)
    each(sum_arrive)

    tot = sums[0]
    for o in range(1, n):
        tot = tot + sums[o]
    sq = jnp.sum(tot[0:1], keepdims=True)
    cross = jnp.sum(tot[1:2], keepdims=True)
    rms = jnp.sqrt(sq / COUNT)
    scale = 1.0 / jnp.maximum(1.0, rms)
    bind = jnp.where(rms > 1.0, 1.0 / (rms * rms * rms), 0.0)
    alpha = jnp.broadcast_to(-0.01 * scale, (STRIP, width))
    beta = jnp.broadcast_to(0.01 * cross * bind / COUNT, (STRIP, width))

    def probe_step(i, _):
        base = pl.multiple_of(i * 512, 512)
        parts = []
        for r in range(0, 512, STRIP):
            rs = pl.ds(pl.multiple_of(base + r, STRIP), STRIP)
            ubar = alpha * adj[rs, :] + beta * upd_s[rs, :]
            parts.append((ubar * k_s[rs, :]).astype(jnp.bfloat16))
        probe_s[...] += dot(tok[:, pl.ds(base, 512)], jnp.concatenate(parts, axis=0))
        return 0

    lax.fori_loop(0, D // 512, probe_step, 0)

    at = lax.broadcasted_iota(jnp.int32, (rows, 128), 0)
    lane = lax.broadcasted_iota(jnp.int32, (rows, 128), 1)

    def score_step(i, _):
        rs = pl.ds(pl.multiple_of(i * rows, rows), rows)
        out = None
        for j in range(width // 128):
            js = slice(j * 128, (j + 1) * 128)
            part = p_s[rs, js] * probe_s[rs, js]
            out = part if out is None else out + part
        total = jnp.sum(out, axis=1, keepdims=True)
        sc[i] = jnp.sum(jnp.where(at == lane, total, 0.0), axis=0, keepdims=True)
        return 0

    lax.fori_loop(0, n, score_step, 0, unroll=4)

    def sc_rows(o):
        return sc.at[o]

    scs[me] = sc[me]

    def score_copy(k):
        o = lax.rem(me + k, n)
        return pltpu.make_async_remote_copy(
            src_ref=sc_rows(o), dst_ref=scs.at[me],
            send_sem=cs.at[k], recv_sem=cr.at[me],
            device_id={"dp": o}, device_id_type=MESH)

    def score_arrive(k):
        o = lax.rem(me + k, n)
        pltpu.make_async_remote_copy(
            src_ref=sc_rows(o), dst_ref=scs.at[o],
            send_sem=cs.at[k], recv_sem=cr.at[o],
            device_id={"dp": o}, device_id_type=MESH).wait_recv()

    each(lambda k: score_copy(k).start())

    def bent_step(i, _):
        rs = pl.ds(pl.multiple_of(i * STRIP, STRIP), STRIP)
        bent_out[rs, :] = (q_s[rs, :] * probe_s[rs, :]).astype(jnp.bfloat16)
        return 0

    lax.fori_loop(0, tokens // STRIP, bent_step, 0, unroll=4)

    def sent_line(i, _):
        o = (i * wide + y) * 2 + core
        for h in range(PIECES):
            @pl.when(i != z)
            def _():
                direct(o, h).wait_send()

            if wide == 2:
                push(2, o, across, h).wait_send()
        return 0

    lax.fori_loop(0, line, sent_line, 0)

    def sent_core(i, _):
        for h in range(PIECES):
            push(3, 2 * i + core, sibling, h).wait_send()
        return 0

    lax.fori_loop(0, n // 2, sent_core, 0)
    each(lambda k: sum_copy(k).wait_send())
    each(score_arrive)
    tot = scs[0]
    for o in range(1, n):
        tot = tot + scs[o]
    score_out[...] = tot
    each(lambda k: score_copy(k).wait_send())
    keep.wait()


def last_kernel(tok_hbm, bent_ref, adj_hbm, sc_ref, theta_hbm, score_ref, tok, adj, theta, tok_sem, adj_sem, out_sem):
    step = D // LAST
    parts = [pl.ds(i * step, step) for i in range(LAST)]
    toks = [pltpu.make_async_copy(tok_hbm.at[:, p], tok.at[:, p], tok_sem.at[i]) for i, p in enumerate(parts)]
    adjs = [pltpu.make_async_copy(adj_hbm.at[p, :], adj.at[p, :], adj_sem.at[i]) for i, p in enumerate(parts)]
    outs = [pltpu.make_async_copy(theta.at[p, :], theta_hbm.at[p, :], out_sem.at[i]) for i, p in enumerate(parts)]
    for i in range(LAST):
        toks[i].start()
        adjs[i].start()

    score_ref[...] = sc_ref[:, :score_ref.shape[1]]

    for i, p in enumerate(parts):
        toks[i].wait()
        adjs[i].wait()
        theta[p, :] = 0.999 * adj[p, :] + dot_rows(tok[:, p], bent_ref[...])
        outs[i].start()
    for copy in outs:
        copy.wait()


def shards(n, wide, x, cotangent, token_weight, weight, moment_one, moment_two, adjoint):
    rows = x.shape[0]
    tokens = n * rows
    width = weight.shape[1]
    f32, bf16 = jnp.float32, jnp.bfloat16
    vm = pl.BlockSpec(memory_space=pltpu.VMEM)
    hbm = pl.BlockSpec(memory_space=pl.ANY)
    dma = pltpu.SemaphoreType.DMA
    tok, bent, sc = pl.pallas_call(
        functools.partial(main_kernel, n, wide),
        out_shape=(
            jax.ShapeDtypeStruct((tokens, D), bf16),
            jax.ShapeDtypeStruct((tokens, width), bf16),
            jax.ShapeDtypeStruct((1, 128), f32),
        ),
        in_specs=[hbm, vm, vm, hbm, hbm, hbm, hbm],
        out_specs=(hbm, vm, vm),
        scratch_shapes=[
            pltpu.VMEM((tokens, D), bf16),
            pltpu.VMEM((D, width), bf16),
            pltpu.VMEM((D, width), bf16),
            pltpu.VMEM((D, width), bf16),
            pltpu.VMEM((D, width), f32),
            pltpu.VMEM((D, width), f32),
            pltpu.VMEM((D, width), f32),
            pltpu.VMEM((tokens, width), f32),
            pltpu.VMEM((tokens, width), f32),
            pltpu.VMEM((tokens, width), f32),
            pltpu.VMEM((tokens, width), bf16),
            pltpu.VMEM((tokens, width), f32),
            pltpu.VMEM((2, 128), f32),
            pltpu.VMEM((n, 2, 128), f32),
            pltpu.VMEM((n, 1, 128), f32),
            pltpu.VMEM((n, 1, 128), f32),
            dma((4,)),
            dma,
            dma,
            dma((4, PIECES, n)),
            dma((PIECES, n)),
            dma((n,)),
            dma((n,)),
            dma((n,)),
            dma((n,)),
        ],
        compiler_params=pltpu.CompilerParams(
            collective_id=0, has_side_effects=True, vmem_limit_bytes=60 * 2**20
        ),
    )(x, cotangent, token_weight.reshape(1, tokens), weight, moment_one, moment_two, adjoint)
    theta, score = pl.pallas_call(
        last_kernel,
        out_shape=(
            jax.ShapeDtypeStruct((D, width), f32),
            jax.ShapeDtypeStruct((1, rows), f32),
        ),
        in_specs=[hbm, vm, hbm, vm],
        out_specs=(hbm, vm),
        scratch_shapes=[
            pltpu.VMEM((tokens, D), bf16),
            pltpu.VMEM((D, width), f32),
            pltpu.VMEM((D, width), f32),
            dma((LAST,)),
            dma((LAST,)),
            dma((LAST,)),
        ],
        compiler_params=pltpu.CompilerParams(vmem_limit_bytes=60 * 2**20),
    )(tok, bent, adjoint, sc)
    return theta, score.reshape(rows)


def solution(mesh):
    n = mesh.shape["dp"]
    wide = 2 if mesh.shape["group"] == 2 else 1
    in_specs = (
        P(("group", "dp"), None),
        P("group", "dp"),
        P("group"),
        P(None, "dp"),
        P(None, "dp"),
        P(None, "dp"),
        P(None, "dp"),
    )
    out_specs = (P("group", "dp"), P(("group", "dp")))
    return jax.shard_map(
        functools.partial(shards, n, wide), mesh=mesh,
        in_specs=in_specs, out_specs=out_specs, check_vma=False)
```
